32 devices in a mesh: doc: 8 (over y, x, core), vocab: 4 (over z).
Axes of the slice: x: 2, y: 2, z: 4, core: 2. Of those that a mesh axis runs over, the one named last changes fastest.
Arguments:
- tile_values: bfloat16 [8, 4, 24, 128, 128], P('doc', 'vocab'), may hold values from -6 to 6
- tile_rows: int32 [8, 4, 24], P('doc', 'vocab'), may hold values from 0 to 7, as said below
- tile_columns: int32 [8, 4, 24], P('doc', 'vocab'), may hold values from 0 to 3
- counts: int32 [8, 4], P('doc', 'vocab'), may hold values from 7 to 24, as said below
- sketch: bfloat16 [2048, 512], P('vocab'), may hold values from -6 to 6
- query_tiles: int32 [2048, 4, 4], P('doc', 'vocab'), may hold values from 0 to 3
- query_values: float32 [2048, 4, 4, 128], P('doc', 'vocab'), may hold values from -6 to 6
Outputs:
- term_basis: float32 [4, 512, 512], P('vocab', 'doc')
- projections: float32 [2048, 512], P('doc')
The draws below stay inside these ranges and needn't reach their ends.
Inputs may be any that keep to these rules, and one draw needn't show every extreme that they name: Each device uses its first counts slots; some device uses all 24 slots in every draw. The (tile_rows, tile_columns) pairs of one device's 24 slots are all different. `query_tiles`: A query may name the same term block more than once; the values then add.
All inputs are finite; a program needn't handle non-finite values.
Results may differ from the reference program's by a relative error of at most 0.0016.
Values may be sent and summed in bfloat16 or wider, within the bound.
No kernel may reach another device: no remote copies, remote signals or barrier semaphores. Data moves between devices by JAX's collectives and lax.ppermute only.
A program may use at most 64 MiB of HBM per device.

```python
import jax
import jax.numpy as jnp
from jax import lax

SKETCH = 512
TILE_EDGE = 128
ROW_TILES = 8
TERM_TILES = 4
QUERY_SLOTS = 4
SLOTS = 24
LOCAL_DOCS = 1024
LOCAL_TERMS = 512
VOCABULARY = 2048
QUERIES = 2048
N_DOC = 8
N_VOCAB = 4


def tile_places(key):
    base_key = jax.random.fold_in(key, 17)
    device_keys = jax.random.split(base_key, N_DOC * N_VOCAB)

    def one_device(device_key):
        return jax.random.permutation(device_key, ROW_TILES * TERM_TILES)[:SLOTS]
    places = jax.vmap(one_device)(device_keys)
    return places.reshape(N_DOC, N_VOCAB, SLOTS).astype(jnp.int32)


def draw_tile_rows(key, part):
    return (tile_places(key) // TERM_TILES).astype(jnp.int32)


def draw_tile_columns(key, part):
    return (tile_places(key) % TERM_TILES).astype(jnp.int32)


def draw_counts(key, part):
    first_key, second_key = jax.random.split(jax.random.fold_in(key, 29))
    uniform_draws = jax.random.randint(first_key, (N_DOC * N_VOCAB,), 0, SLOTS + 1, dtype=jnp.int32)
    slot_loads = jnp.maximum(uniform_draws * uniform_draws // SLOTS, SLOTS // 4 + 1)
    busiest = jax.random.randint(second_key, (), 0, N_DOC * N_VOCAB, dtype=jnp.int32)
    positions = jnp.arange(N_DOC * N_VOCAB, dtype=jnp.int32)
    slot_loads = jnp.where(positions == busiest, SLOTS, slot_loads)
    return slot_loads.reshape(N_DOC, N_VOCAB).astype(jnp.int32)


def plant(entries, own_key, smallest, high):
    shape = entries.shape
    spot = [jax.random.randint(jax.random.fold_in(own_key, axis), (), 0, shape[axis]) for axis in range(len(shape))]
    entries = entries.at[tuple(spot)].set(smallest)
    longest = shape.index(max(shape))
    spot[longest] = (spot[longest] + 1) % shape[longest]
    return entries.at[tuple(spot)].set(high)


def block_scale(key, extent, cuts, least, top_value):
    loudness, own = 1.0, jax.random.fold_in(key, 6)
    for axis_at, blocks in cuts:
        steps = jnp.exp(jax.random.uniform(jax.random.fold_in(own, axis_at), (blocks,), jnp.float32, least / len(cuts), top_value / len(cuts)))
        loudness = loudness * jnp.repeat(steps, extent[axis_at] // blocks).reshape([-1 if axis == axis_at else 1 for axis in range(len(extent))])
    return loudness


def gaussian(rng, extent, deviation, most, cuts=(), kind=jnp.bfloat16):
    loudness = block_scale(rng, extent, cuts, -0.22, 0.18) if cuts else 1.0
    entries = jax.random.normal(rng, extent, jnp.float32) * deviation * loudness
    return jnp.minimum(jnp.maximum(entries, -most), most).astype(kind)


def setup_inputs(seed: int = 0) -> dict:
    keys = jax.random.split(jax.random.key(seed), 8)
    tile_values = gaussian(keys[0], (N_DOC, N_VOCAB, SLOTS, TILE_EDGE, TILE_EDGE), 1.0, 6.0, ((0, 8), (1, 4)))
    tile_rows = draw_tile_rows(jax.random.fold_in(keys[7], 71), 0)
    tile_columns = draw_tile_columns(jax.random.fold_in(keys[7], 71), 0)
    counts = draw_counts(jax.random.fold_in(keys[7], 71), 0)
    sketch = gaussian(keys[4], (VOCABULARY, SKETCH), 1.0, 6.0, ((0, 4),))
    query_tiles = plant(jax.random.randint(keys[5], (QUERIES, N_VOCAB, QUERY_SLOTS), 0, TERM_TILES), jax.random.fold_in(keys[5], 1), 0, TERM_TILES - 1).astype(jnp.int32)
    query_values = gaussian(keys[6], (QUERIES, N_VOCAB, QUERY_SLOTS, TILE_EDGE), 1.0, 6.0, ((0, 8), (1, 4)), jnp.float32)
    return {"tile_values": tile_values, "tile_rows": tile_rows, "tile_columns": tile_columns, "counts": counts, "sketch": sketch, "query_tiles": query_tiles, "query_values": query_values}


precise = lax.Precision.HIGHEST

def reference(tile_values, tile_rows, tile_columns, counts, sketch, query_tiles, query_values):
    slot_index = jnp.arange(SLOTS, dtype=jnp.int32)
    row_ids = jnp.arange(ROW_TILES, dtype=jnp.int32)
    term_ids = jnp.arange(TERM_TILES, dtype=jnp.int32)
    sketch_blocks = sketch.astype(jnp.float32).reshape(N_VOCAB, TERM_TILES, TILE_EDGE, SKETCH)

    def forward_device(inputs):
        blocks, at_rows, at_columns, used_slots, own_sketch = inputs
        active = (slot_index < used_slots).astype(jnp.float32)
        product = jnp.einsum('sij,sjk->sik', blocks.astype(jnp.float32), own_sketch[at_columns], precision=precise)
        placing = (at_rows[:, None] == row_ids[None, :]).astype(jnp.float32) * active[:, None]
        return jnp.einsum('sr,sik->rik', placing, product, precision=precise)

    def forward_document(inputs):
        blocks, at_rows, at_columns, used_slots = inputs
        pieces = lax.map(forward_device, (blocks, at_rows, at_columns, used_slots, sketch_blocks))
        return lax.optimization_barrier(jnp.sum(pieces, axis=0)).reshape(LOCAL_DOCS, SKETCH).astype(jnp.bfloat16)
    sketched = lax.map(forward_document, (tile_values, tile_rows, tile_columns, counts))

    def backward_document(totals, inputs):
        blocks, at_rows, at_columns, used_slots, document_rows = inputs
        row_blocks = document_rows.astype(jnp.float32).reshape(ROW_TILES, TILE_EDGE, SKETCH)

        def backward_device(device_inputs):
            device_blocks, device_rows, device_columns, device_used = device_inputs
            active = (slot_index < device_used).astype(jnp.float32)
            product = jnp.einsum('sij,sik->sjk', device_blocks.astype(jnp.float32), row_blocks[device_rows], precision=precise)
            placing = (device_columns[:, None] == term_ids[None, :]).astype(jnp.float32) * active[:, None]
            return jnp.einsum('sc,sjk->cjk', placing, product, precision=precise).reshape(LOCAL_TERMS, SKETCH)
        pieces = lax.map(backward_device, (blocks, at_rows, at_columns, used_slots))
        return (totals + pieces, None)
    start_back = jnp.zeros((N_VOCAB, LOCAL_TERMS, SKETCH), jnp.float32)
    back, _ = lax.scan(backward_document, start_back, (tile_values, tile_rows, tile_columns, counts, sketched))
    term_matrix = back.reshape(VOCABULARY, SKETCH)
    gram = jnp.dot(term_matrix.T, term_matrix, precision=precise)
    factor = jnp.linalg.cholesky(gram / VOCABULARY)
    term_basis = lax.linalg.triangular_solve(factor, term_matrix, left_side=False, lower=True, transpose_a=True)

    def project(running, vocab_index):
        tiles_here = lax.dynamic_index_in_dim(query_tiles, vocab_index, 1, keepdims=False)
        values_here = lax.dynamic_index_in_dim(query_values, vocab_index, 1, keepdims=False)
        onehot = (tiles_here[:, :, None] == term_ids[None, None, :]).astype(jnp.float32)
        dense_here = jnp.einsum('qtc,qti->qci', onehot, values_here, precision=precise).reshape(QUERIES, LOCAL_TERMS)
        basis_here = lax.dynamic_slice_in_dim(term_basis, (vocab_index * LOCAL_TERMS).astype(jnp.int32), LOCAL_TERMS, 0)
        return (running + jnp.dot(dense_here, basis_here, precision=precise), None)
    raw, _ = lax.scan(project, jnp.zeros((QUERIES, SKETCH), jnp.float32), jnp.arange(N_VOCAB, dtype=jnp.int32))
    projections = raw * lax.rsqrt(lax.optimization_barrier(jnp.mean(raw * raw, axis=1, keepdims=True)) + 1e-06)
    return (term_basis.reshape(N_VOCAB, LOCAL_TERMS, SKETCH), projections)
```

```python
import functools

import jax
import jax.numpy as jnp
from jax import lax
from jax.experimental import pallas as pl
from jax.experimental.pallas import tpu as pltpu
from jax.sharding import PartitionSpec as P


ROW_TILES = 8
PANEL = 32
TILE = 128
CORES = 2

precise = lax.Precision.HIGHEST
smem = pl.BlockSpec(memory_space=pltpu.SMEM)
vmem = pl.BlockSpec(memory_space=pltpu.VMEM)
f32 = jnp.float32
bf16 = jnp.bfloat16


def dot(left, right, dims, precision=None):
    return lax.dot_general(
        left, right, (dims, ((), ())), precision=precision, preferred_element_type=f32
    )


def invert_factor(work):
    tiles = work.shape[0] // TILE
    chunks = PANEL // 8
    panels = TILE // PANEL
    sub_id = lax.broadcasted_iota(jnp.int32, (8, TILE), 0)
    lane_id = lax.broadcasted_iota(jnp.int32, (8, TILE), 1)

    def block(o, carry):
        base = pl.multiple_of(o * TILE, TILE)
        for s in range(panels):
            lo = s * PANEL
            at = base + lo
            own = [work[pl.ds(at + 8 * r, 8), pl.ds(base, TILE)] for r in range(chunks)]
            col = [[None] * chunks for _ in range(PANEL)]
            for l in range(PANEL):
                for r in range(l // 8, chunks):
                    col[l][r] = jnp.broadcast_to(own[r][:, lo + l : lo + l + 1], (8, TILE))
            in_panel = (lane_id >= lo) & (lane_id < lo + PANEL)
            rows = []
            for r in range(chunks):
                eye = (lane_id == lo + 8 * r + sub_id).astype(f32)
                line = []
                for t in range(tiles):
                    old = work[pl.ds(at + 8 * r, 8), t * TILE : (t + 1) * TILE]
                    line.append(jnp.where(in_panel & (o == t), eye, old))
                rows.append(line)
            for k in range(PANEL):
                kr, ks = k // 8, k % 8
                pivot = jnp.broadcast_to(col[k][kr][ks : ks + 1, :], (8, TILE))
                q = lax.rsqrt(pivot)
                lcol = [None] * chunks
                for r in range(kr, chunks):
                    lcol[r] = col[k][r] * q
                for l in range(k + 1, PANEL):
                    e = jnp.broadcast_to(lcol[l // 8][l % 8 : l % 8 + 1, :], (8, TILE))
                    for r in range(l // 8, chunks):
                        col[l][r] = col[l][r] - lcol[r] * e
                below = jnp.where(sub_id > ks, lcol[kr], 0.0)
                for t in range(tiles):
                    rk = jnp.broadcast_to(rows[kr][t][ks : ks + 1, :], (8, TILE)) * q
                    rows[kr][t] = jnp.where(sub_id == ks, rk, rows[kr][t] - below * rk)
                    for r in range(kr + 1, chunks):
                        rows[r][t] = rows[r][t] - lcol[r] * rk
            for r in range(chunks):
                for t in range(tiles):
                    work[pl.ds(at + 8 * r, 8), t * TILE : (t + 1) * TILE] = rows[r][t]
            if s + 1 < panels:
                left = work[pl.ds(at, PANEL), pl.ds(base, TILE)]
                full = work[pl.ds(at, PANEL), :]
                update = dot(left, full, ((0,), (0,)), precise)
                first = lo + PANEL
                count = TILE - first
                lanes = lax.broadcasted_iota(jnp.int32, (count, TILE), 1)
                gone = (lanes >= lo) & (lanes < lo + PANEL)
                for t in range(tiles):
                    span = slice(t * TILE, (t + 1) * TILE)
                    old = work[pl.ds(base + first, count), span]
                    old = jnp.where(gone & (o == t), 0.0, old)
                    work[pl.ds(base + first, count), span] = old - update[first:, span]
        square = work[pl.ds(base, TILE), pl.ds(base, TILE)]
        lower = lax.broadcasted_iota(jnp.int32, (TILE, TILE), 0) >= lax.broadcasted_iota(
            jnp.int32, (TILE, TILE), 1
        )
        work[pl.ds(base, TILE), pl.ds(base, TILE)] = jnp.where(lower, square, 0.0)

        def later(b, inner):
            below_at = pl.multiple_of(b * TILE, TILE)
            left = work[pl.ds(base, TILE), pl.ds(below_at, TILE)]
            update = dot(left, work[pl.ds(base, TILE), :], ((0,), (0,)), precise)
            work[pl.ds(below_at, TILE), pl.ds(base, TILE)] = jnp.zeros((TILE, TILE), f32)
            work[pl.ds(below_at, TILE), :] = work[pl.ds(below_at, TILE), :] - update
            return inner

        lax.fori_loop(o + 1, tiles, later, 0)
        return carry

    lax.fori_loop(0, tiles, block, 0)


def dense_kernel(where, at_rows, at_columns, used, tiles, *refs):
    outs, dense = refs[:-1], refs[-1]
    parts = len(outs)
    rows = dense.shape[0] // parts
    dense[...] = jnp.zeros_like(dense)

    def place(s, carry):
        r = pl.multiple_of(at_rows[0, s] * TILE, TILE)
        c = pl.multiple_of(at_columns[0, s] * TILE, TILE)
        dense[pl.ds(r, TILE), pl.ds(c, TILE)] = tiles[s]
        return carry

    lax.fori_loop(0, used[0, 0], place, 0)
    for s in range(parts):
        at = pl.multiple_of(lax.rem(where[0] + s, parts) * rows, rows)
        outs[s][...] = dense[pl.ds(at, rows), :]


def forward_kernel(where, parts, places, *refs):
    blocks = refs[:parts]
    own_sketch = refs[parts]
    pieces = refs[parts + 1 : parts + 1 + len(places)]
    out, full = refs[-2], refs[-1]
    rows = pieces[0].shape[1]
    for piece, place in zip(pieces, places):
        at = pl.multiple_of(lax.bitwise_xor(where[1], place) * rows, rows)
        for s in range(parts - 1):
            full[s, pl.ds(at, rows), :] = piece[s]
    total = dot(blocks[0][...], own_sketch[...], ((1,), (0,)))
    for s in range(1, parts):
        total = total + dot(blocks[s][...], full[s - 1], ((1,), (0,)))
    out[...] = total.astype(bf16)


def backward_kernel(where, parts, places, *refs):
    dense = refs[:parts]
    sketched = refs[parts : 2 * parts]
    outs = refs[2 * parts : -1]
    full = refs[-1]
    total = dot(dense[0][...], sketched[0][...], ((0,), (0,)))
    for s in range(1, parts):
        total = total + dot(dense[parts - s][...], sketched[s][...], ((0,), (0,)))
    full[...] = total
    rows = outs[0].shape[0]
    for out, place in zip(outs, places):
        at = pl.multiple_of(lax.bitwise_xor(where[1], place) * rows, rows)
        out[...] = full[pl.ds(at, rows), :]


def gram_kernel(where, places, *refs):
    pieces = refs[: len(places)]
    gram, back, product = refs[len(places) :]
    rows = pieces[0].shape[0]
    for piece, place in zip(pieces, places):
        at = pl.multiple_of(lax.bitwise_xor(where[1], place) * rows, rows)
        back[pl.ds(at, rows), :] = piece[...]
    share = gram.shape[0]
    start = where[1] * share
    tile_at = pl.multiple_of(start // TILE * TILE, TILE)
    product[...] = dot(back[:, pl.ds(tile_at, TILE)], back[...], ((0,), (0,)), precise)
    gram[...] = product[pl.ds(pl.multiple_of(start - tile_at, share), share), :]


def query_kernel(where, tiles, values, back, *refs):
    outs, full = refs[:-1], refs[-1]
    slots = tiles.shape[1]
    columns = []
    for c in range(back.shape[0] // TILE):
        total = None
        for j in range(slots):
            part = jnp.where(tiles[:, j : j + 1] == c, values[:, j * TILE : (j + 1) * TILE], 0.0)
            total = part if total is None else total + part
        columns.append(total)
    full[...] = dot(jnp.concatenate(columns, axis=1), back[...], ((1,), (0,)), precise)
    parts = len(outs)
    rows = outs[0].shape[0]
    for s in range(parts):
        at = pl.multiple_of(lax.rem(where[0] + s, parts) * rows, rows)
        outs[s][...] = full[pl.ds(at, rows), :]


def ordered_sum_kernel(where, parts, *refs):
    pieces, out, stack = refs[:parts], refs[-2], refs[-1]
    for s in range(parts):
        stack[lax.rem(where[0] + parts - s, parts)] = pieces[s][...]
    total = stack[0]
    for s in range(1, parts):
        total = total + stack[s]
    out[...] = total


def factor_kernel(where, places, scale, *refs):
    pieces, out, work = refs[: len(places)], refs[-2], refs[-1]
    rows = pieces[0].shape[0]
    for piece, place in zip(pieces, places):
        at = pl.multiple_of(lax.bitwise_xor(where[1], place) * rows, rows)
        work[pl.ds(at, rows), :] = piece[...] * scale
    invert_factor(work)
    n = work.shape[0]
    lower = lax.broadcasted_iota(jnp.int32, (n, n), 0) >= lax.broadcasted_iota(jnp.int32, (n, n), 1)
    out[...] = jnp.where(lower, work[...], 0.0)


def output_kernel(where, parts, *refs):
    inverse, own = refs[0], refs[1]
    coords = refs[2 : 2 + parts]
    basis, projections, full = refs[2 + parts :]
    rows = coords[0].shape[0]
    for s in range(parts):
        at = pl.multiple_of(lax.rem(where[0] + parts - s, parts) * rows, rows)
        full[pl.ds(at, rows), :] = coords[s][...]
    basis[...] = dot(own[...], inverse[...], ((1,), (1,)), precise)
    raw = dot(full[...], inverse[...], ((1,), (1,)), precise)
    mean = jnp.sum(raw * raw, axis=1, keepdims=True) * (1.0 / raw.shape[1])
    projections[...] = raw * lax.rsqrt(mean + 1e-06)


def call(kernel, name, outs, scratch, scalars, arrays):
    return pl.pallas_call(
        kernel,
        out_shape=outs,
        in_specs=[smem] * len(scalars) + [vmem] * len(arrays),
        out_specs=jax.tree.map(lambda _: vmem, outs),
        scratch_shapes=scratch,
        name=name,
    )(*scalars, *arrays)


def body(tile_values, tile_rows, tile_columns, counts, sketch, query_tiles, query_values):
    n_doc, n_vocab = lax.axis_size("doc"), lax.axis_size("vocab")
    doc, vocab = lax.axis_index("doc"), lax.axis_index("vocab")
    where = jnp.stack([vocab, doc]).astype(jnp.int32)
    chips = n_doc // CORES
    _, _, slots, edge, _ = tile_values.shape
    terms, width = sketch.shape
    queries = query_tiles.shape[0]
    documents = ROW_TILES * edge
    share = terms // n_doc
    shifts = range(1, n_vocab)
    places = [CORES * m + c for m in range(chips) for c in range(CORES)]

    def along(x, shift):
        return lax.ppermute(x, "vocab", [(a, (a + shift) % n_vocab) for a in range(n_vocab)])

    def across(x, place):
        return lax.ppermute(x, "doc", [(a, a ^ place) for a in range(n_doc)])

    def spread(x):
        near = [x] + [across(x, CORES * m) for m in range(1, chips)]
        far = [across(piece, 1) for piece in near]
        return [piece for pair in zip(near, far) for piece in pair]

    own_terms = lax.dynamic_slice_in_dim(sketch, doc * share, share, 0)
    others = jnp.stack([along(own_terms, s) for s in shifts])
    sketch_pieces = spread(others)

    rows = documents // n_vocab
    dense = call(
        dense_kernel,
        "dense",
        [jax.ShapeDtypeStruct((rows, terms), bf16)] * n_vocab,
        [pltpu.VMEM((documents, terms), bf16)],
        [where, tile_rows[0], tile_columns[0], counts],
        [tile_values[0, 0]],
    )
    blocks = [dense[0]] + [along(dense[s], s) for s in shifts]
    own_sketched = call(
        lambda where, *refs: forward_kernel(where, n_vocab, places, *refs),
        "forward",
        jax.ShapeDtypeStruct((rows, width), bf16),
        [pltpu.VMEM((n_vocab - 1, terms, width), bf16)],
        [where],
        [*blocks, sketch, *sketch_pieces],
    )
    sketched = [own_sketched] + [along(own_sketched, s) for s in shifts]
    piece = jax.ShapeDtypeStruct((share, width), f32)
    parted = call(
        lambda where, *refs: backward_kernel(where, n_vocab, places, *refs),
        "backward",
        [piece] * n_doc,
        [pltpu.VMEM((terms, width), f32)],
        [where],
        [*dense, *sketched],
    )
    paired = [parted[CORES * m] + across(parted[CORES * m + 1], 1) for m in range(chips)]
    own_back = paired[0]
    for m in range(1, chips):
        own_back = own_back + across(paired[m], CORES * m)
    back_pieces = spread(own_back)
    gram_share = width // n_doc
    gram_part, back = call(
        lambda where, *refs: gram_kernel(where, places, *refs),
        "gram",
        [
            jax.ShapeDtypeStruct((gram_share, width), f32),
            jax.ShapeDtypeStruct((terms, width), f32),
        ],
        [pltpu.VMEM((TILE, width), f32)],
        [where],
        back_pieces,
    )
    gram_parts = [gram_part] + [along(gram_part, s) for s in shifts]
    query_rows = queries // n_vocab
    query_parts = call(
        query_kernel,
        "query",
        [jax.ShapeDtypeStruct((query_rows, width), f32)] * n_vocab,
        [pltpu.VMEM((queries, width), f32)],
        [where],
        [query_tiles[:, 0], query_values.reshape(queries, -1), back],
    )
    gram_rows = call(
        lambda where, *refs: ordered_sum_kernel(where, n_vocab, *refs),
        "gram_sum",
        jax.ShapeDtypeStruct((gram_share, width), f32),
        [pltpu.VMEM((n_vocab, gram_share, width), f32)],
        [where],
        gram_parts,
    )
    gram_pieces = spread(gram_rows)
    own_query = query_parts[0]
    for s in shifts:
        own_query = own_query + along(query_parts[s], s)
    coords = [own_query] + [along(own_query, s) for s in shifts]
    inverse = call(
        lambda where, *refs: factor_kernel(where, places, 1.0 / (terms * n_vocab), *refs),
        "factor",
        jax.ShapeDtypeStruct((width, width), f32),
        [pltpu.VMEM((width, width), f32)],
        [where],
        gram_pieces,
    )
    basis, projections = call(
        lambda where, *refs: output_kernel(where, n_vocab, *refs),
        "output",
        [
            jax.ShapeDtypeStruct((share, width), f32),
            jax.ShapeDtypeStruct((queries, width), f32),
        ],
        [pltpu.VMEM((queries, width), f32)],
        [where],
        [inverse, own_back, *coords],
    )
    return basis[None], projections


def solution(mesh):
    return jax.shard_map(
        body,
        mesh=mesh,
        in_specs=(
            P("doc", "vocab", None, None, None),
            P("doc", "vocab", None),
            P("doc", "vocab", None),
            P("doc", "vocab"),
            P("vocab", None),
            P("doc", "vocab", None),
            P("doc", "vocab", None, None),
        ),
        out_specs=(P("vocab", "doc", None), P("doc", None)),
        check_vma=False,
    )
```

```python
import jax
import jax.numpy as jnp
from jax import lax
from jax.experimental import pallas as pl
from jax.experimental.pallas import tpu as pltpu
from jax.sharding import PartitionSpec as P


ROW_TILES = 8
PANEL = 32
TILE = 128
CORES = 2
HALVES = 2

precise = lax.Precision.HIGHEST
smem = pl.BlockSpec(memory_space=pltpu.SMEM)
vmem = pl.BlockSpec(memory_space=pltpu.VMEM)
f32 = jnp.float32
bf16 = jnp.bfloat16


def dot(left, right, dims, precision=None):
    return lax.dot_general(
        left, right, (dims, ((), ())), precision=precision, preferred_element_type=f32
    )


def invert_factor(work):
    tiles = work.shape[0] // TILE
    chunks = PANEL // 8
    panels = TILE // PANEL
    sub_id = lax.broadcasted_iota(jnp.int32, (8, TILE), 0)
    lane_id = lax.broadcasted_iota(jnp.int32, (8, TILE), 1)

    def block(o, carry):
        base = pl.multiple_of(o * TILE, TILE)
        for s in range(panels):
            lo = s * PANEL
            at = base + lo
            own = [work[pl.ds(at + 8 * r, 8), pl.ds(base, TILE)] for r in range(chunks)]
            col = [[None] * chunks for _ in range(PANEL)]
            for l in range(PANEL):
                for r in range(l // 8, chunks):
                    col[l][r] = jnp.broadcast_to(own[r][:, lo + l : lo + l + 1], (8, TILE))
            in_panel = (lane_id >= lo) & (lane_id < lo + PANEL)
            rows = []
            for r in range(chunks):
                eye = (lane_id == lo + 8 * r + sub_id).astype(f32)
                line = []
                for t in range(tiles):
                    old = work[pl.ds(at + 8 * r, 8), t * TILE : (t + 1) * TILE]
                    line.append(jnp.where(in_panel & (o == t), eye, old))
                rows.append(line)
            for k in range(PANEL):
                kr, ks = k // 8, k % 8
                pivot = jnp.broadcast_to(col[k][kr][ks : ks + 1, :], (8, TILE))
                q = lax.rsqrt(pivot)
                lcol = [None] * chunks
                for r in range(kr, chunks):
                    lcol[r] = col[k][r] * q
                for l in range(k + 1, PANEL):
                    e = jnp.broadcast_to(lcol[l // 8][l % 8 : l % 8 + 1, :], (8, TILE))
                    for r in range(l // 8, chunks):
                        col[l][r] = col[l][r] - lcol[r] * e
                below = jnp.where(sub_id > ks, lcol[kr], 0.0)
                for t in range(tiles):
                    rk = jnp.broadcast_to(rows[kr][t][ks : ks + 1, :], (8, TILE)) * q
                    rows[kr][t] = jnp.where(sub_id == ks, rk, rows[kr][t] - below * rk)
                    for r in range(kr + 1, chunks):
                        rows[r][t] = rows[r][t] - lcol[r] * rk
            for r in range(chunks):
                for t in range(tiles):
                    work[pl.ds(at + 8 * r, 8), t * TILE : (t + 1) * TILE] = rows[r][t]
            if s + 1 < panels:
                left = work[pl.ds(at, PANEL), pl.ds(base, TILE)]
                full = work[pl.ds(at, PANEL), :]
                update = dot(left, full, ((0,), (0,)), precise)
                first = lo + PANEL
                count = TILE - first
                lanes = lax.broadcasted_iota(jnp.int32, (count, TILE), 1)
                gone = (lanes >= lo) & (lanes < lo + PANEL)
                for t in range(tiles):
                    span = slice(t * TILE, (t + 1) * TILE)
                    old = work[pl.ds(base + first, count), span]
                    old = jnp.where(gone & (o == t), 0.0, old)
                    work[pl.ds(base + first, count), span] = old - update[first:, span]
        square = work[pl.ds(base, TILE), pl.ds(base, TILE)]
        lower = lax.broadcasted_iota(jnp.int32, (TILE, TILE), 0) >= lax.broadcasted_iota(
            jnp.int32, (TILE, TILE), 1
        )
        work[pl.ds(base, TILE), pl.ds(base, TILE)] = jnp.where(lower, square, 0.0)

        def later(b, inner):
            below_at = pl.multiple_of(b * TILE, TILE)
            left = work[pl.ds(base, TILE), pl.ds(below_at, TILE)]
            update = dot(left, work[pl.ds(base, TILE), :], ((0,), (0,)), precise)
            work[pl.ds(below_at, TILE), pl.ds(base, TILE)] = jnp.zeros((TILE, TILE), f32)
            work[pl.ds(below_at, TILE), :] = work[pl.ds(below_at, TILE), :] - update
            return inner

        lax.fori_loop(o + 1, tiles, later, 0)
        return carry

    lax.fori_loop(0, tiles, block, 0)


def dense_kernel(where, halves, places, at_rows, at_columns, used, tiles, *refs):
    outs, dense = refs[:-1], refs[-1]
    rows = dense.shape[0] // len(outs)
    dense[...] = jnp.zeros_like(dense)

    def place(s, carry):
        r = pl.multiple_of(at_rows[0, s] * TILE, TILE)
        c = pl.multiple_of(at_columns[0, s] * TILE, TILE)
        dense[pl.ds(r, TILE), pl.ds(c, TILE)] = tiles[s]
        return carry

    lax.fori_loop(0, used[0, 0], place, 0)
    for i, out in enumerate(outs):
        block = lax.bitwise_xor(where[0], places[i // halves]) * halves + i % halves
        out[...] = dense[pl.ds(pl.multiple_of(block * rows, rows), rows), :]


def turn_kernel(*refs):
    blocks, out = refs[:-1], refs[-1]
    whole = jnp.concatenate([block[...] for block in blocks], axis=0)
    out[...] = whole.T


def assemble_kernel(where, places, *refs):
    pieces, out = refs[:-1], refs[-1]
    rows = pieces[0].shape[1]
    for piece, place in zip(pieces, places):
        at = pl.multiple_of(lax.bitwise_xor(where[1], place) * rows, rows)
        out[:, pl.ds(at, rows), :] = piece[...]


def forward_kernel(*refs):
    blocks = refs[:-3]
    own_sketch, others, out = refs[-3:]
    total = dot(blocks[0][...], own_sketch[...], ((1,), (0,)))
    for s in range(1, len(blocks)):
        total = total + dot(blocks[s][...], others[s - 1], ((1,), (0,)))
    out[...] = total.astype(bf16)


def backward_kernel(where, places, turned, *refs):
    outs = refs[-2 - len(places) : -2]
    sketched = refs[: -2 - len(places)]
    whole, full = refs[-2:]
    height = sketched[0].shape[0]
    for i, piece in enumerate(sketched):
        whole[i * height : (i + 1) * height, :] = piece[...]
    full[...] = dot(turned[...], whole[...], ((1,), (0,)))
    rows = outs[0].shape[0]
    for out, place in zip(outs, places):
        at = pl.multiple_of(lax.bitwise_xor(where[1], place) * rows, rows)
        out[...] = full[pl.ds(at, rows), :]


def gram_kernel(where, places, *refs):
    pieces = refs[: len(places)]
    gram, back, product = refs[len(places) :]
    rows = pieces[0].shape[0]
    for i, piece in enumerate(pieces):
        back[i * rows : (i + 1) * rows, :] = piece[...]
    share = gram.shape[0]
    start = where[1] * share
    tile_at = pl.multiple_of(start // TILE * TILE, TILE)
    product[...] = dot(back[:, pl.ds(tile_at, TILE)], back[...], ((0,), (0,)), precise)
    gram[...] = product[pl.ds(pl.multiple_of(start - tile_at, share), share), :]


def query_dense_kernel(tiles, values, out):
    for c in range(out.shape[1] // TILE):
        total = None
        for j in range(tiles.shape[1]):
            part = jnp.where(tiles[:, j : j + 1] == c, values[:, j * TILE : (j + 1) * TILE], 0.0)
            total = part if total is None else total + part
        out[:, c * TILE : (c + 1) * TILE] = total


def query_kernel(where, places, v_places, dense, *refs):
    pieces = refs[: len(places)]
    outs = refs[len(places) : -2]
    back, full = refs[-2:]
    height = pieces[0].shape[0]
    for piece, place in zip(pieces, places):
        at = pl.multiple_of(lax.bitwise_xor(where[1], place) * height, height)
        back[pl.ds(at, height), :] = piece[...]
    full[...] = dot(dense[...], back[...], ((1,), (0,)), precise)
    rows = outs[0].shape[0]
    for out, place in zip(outs, v_places):
        at = pl.multiple_of(lax.bitwise_xor(where[0], place) * rows, rows)
        out[...] = full[pl.ds(at, rows), :]


def factor_kernel(where, places, scale, *refs):
    pieces, out, work = refs[: len(places)], refs[-2], refs[-1]
    rows = pieces[0].shape[0]
    for piece, place in zip(pieces, places):
        at = pl.multiple_of(lax.bitwise_xor(where[1], place) * rows, rows)
        work[pl.ds(at, rows), :] = piece[...] * scale
    invert_factor(work)
    n = work.shape[0]
    lower = lax.broadcasted_iota(jnp.int32, (n, n), 0) >= lax.broadcasted_iota(jnp.int32, (n, n), 1)
    out[...] = jnp.where(lower, work[...], 0.0)


def output_kernel(where, v_places, *refs):
    inverse, own = refs[0], refs[1]
    coords = refs[2 : 2 + len(v_places)]
    basis, projections, full = refs[2 + len(v_places) :]
    rows = coords[0].shape[0]
    for piece, place in zip(coords, v_places):
        at = pl.multiple_of(lax.bitwise_xor(where[0], place) * rows, rows)
        full[pl.ds(at, rows), :] = piece[...]
    basis[...] = dot(own[...], inverse[...], ((1,), (1,)), precise)
    raw = dot(full[...], inverse[...], ((1,), (1,)), precise)
    mean = jnp.sum(raw * raw, axis=1, keepdims=True) * (1.0 / raw.shape[1])
    projections[...] = raw * lax.rsqrt(mean + 1e-06)


def call(kernel, outs, scratch, scalars, arrays, keep=True):
    if keep:
        outs = jax.tree.map(lambda x: pltpu.VMEM(x.shape, x.dtype), outs)
    return pl.pallas_call(
        kernel,
        out_shape=outs,
        in_specs=[smem] * len(scalars) + [vmem] * len(arrays),
        out_specs=jax.tree.map(lambda _: vmem, outs),
        scratch_shapes=scratch,
        compiler_params=pltpu.CompilerParams(vmem_limit_bytes=16 << 20),
    )(*scalars, *[pltpu.with_memory_space_constraint(x, pltpu.VMEM) for x in arrays])


def work(tile_values, tile_rows, tile_columns, counts, sketch, query_tiles, query_values):
    n_doc, n_vocab = lax.axis_size("doc"), lax.axis_size("vocab")
    doc, vocab = lax.axis_index("doc"), lax.axis_index("vocab")
    where = jnp.stack([vocab, doc]).astype(jnp.int32)
    chips = n_doc // CORES
    edge = tile_values.shape[3]
    terms, width = sketch.shape
    queries = query_tiles.shape[0]
    documents = ROW_TILES * edge
    share = terms // n_doc
    places = [CORES * m + c for m in range(chips) for c in range(CORES)]
    bits = [1 << b for b in reversed(range(n_vocab.bit_length() - 1))]
    v_places = [0]
    for bit in bits:
        v_places += [place | bit for place in v_places]

    def along(x, place):
        return lax.ppermute(x, "vocab", [(a, a ^ place) for a in range(n_vocab)])

    def across(x, place):
        return lax.ppermute(x, "doc", [(a, a ^ place) for a in range(n_doc)])

    def collect(x):
        held = [x]
        for bit in bits:
            near = along(x, bit)
            held += [near] + [along(piece, bit) for piece in held[1:]]
        return held

    def spread(x):
        near = [x]
        for m in range(1, chips):
            near.append(across(x, CORES * m))
        far = [across(piece, 1) for piece in near]
        return [piece for pair in zip(near, far) for piece in pair]

    rows = documents // n_vocab // HALVES
    dense = call(
        lambda where, *refs: dense_kernel(where, HALVES, v_places, *refs),
        [jax.ShapeDtypeStruct((rows, terms), bf16)] * (n_vocab * HALVES),
        [pltpu.VMEM((documents, terms), bf16)],
        [where, tile_rows[0], tile_columns[0], counts],
        [tile_values[0, 0]],
    )
    own_terms = lax.dynamic_slice_in_dim(sketch, doc * share, share, 0)
    blocks = [
        [dense[h]] + [along(dense[i * HALVES + h], v_places[i]) for i in range(1, n_vocab)]
        for h in range(HALVES)
    ]
    others = jnp.stack([along(own_terms, place) for place in v_places[1:]])
    term_pieces = spread(others)
    other_sketch = call(
        lambda where, *refs: assemble_kernel(where, places, *refs),
        jax.ShapeDtypeStruct((n_vocab - 1, terms, width), bf16),
        [],
        [where],
        term_pieces,
    )
    turned = call(turn_kernel, jax.ShapeDtypeStruct((terms, documents), bf16), [], [], dense)
    query_dense = call(
        query_dense_kernel,
        jax.ShapeDtypeStruct((queries, terms), f32),
        [],
        [],
        [query_tiles[:, 0], query_values.reshape(queries, -1)],
    )
    gathered = []
    for h in range(HALVES):
        own_sketched = call(
            forward_kernel,
            jax.ShapeDtypeStruct((rows, width), bf16),
            [],
            [],
            [*blocks[h], sketch, other_sketch],
        )
        gathered.append(collect(own_sketched))
    sketched = [gathered[h][i] for i in range(n_vocab) for h in range(HALVES)]
    piece = jax.ShapeDtypeStruct((share, width), f32)
    parted = call(
        lambda where, *refs: backward_kernel(where, places, *refs),
        [piece] * n_doc,
        [pltpu.VMEM((documents, width), bf16), pltpu.VMEM((terms, width), f32)],
        [where],
        [turned, *sketched],
    )
    paired = [parted[CORES * m] + across(parted[CORES * m + 1], 1) for m in range(chips)]
    own_back = paired[0]
    for m in range(1, chips):
        own_back = own_back + across(paired[m], CORES * m)
    back_pieces = spread(own_back)
    gram_share = width // n_doc
    gram_rows = call(
        lambda where, *refs: gram_kernel(where, places, *refs),
        jax.ShapeDtypeStruct((gram_share, width), f32),
        [pltpu.VMEM((terms, width), f32), pltpu.VMEM((TILE, width), f32)],
        [where],
        back_pieces,
    )
    for bit in reversed(bits):
        gram_rows = gram_rows + along(gram_rows, bit)
    query_rows = queries // n_vocab
    query_parts = call(
        lambda where, *refs: query_kernel(where, places, v_places, *refs),
        [jax.ShapeDtypeStruct((query_rows, width), f32)] * n_vocab,
        [pltpu.VMEM((terms, width), f32), pltpu.VMEM((queries, width), f32)],
        [where],
        [query_dense, *back_pieces],
    )
    gram_pieces = spread(gram_rows)
    own_query = query_parts[0]
    for i in range(1, n_vocab):
        own_query = own_query + along(query_parts[i], v_places[i])
    coords = [own_query] + [along(own_query, place) for place in v_places[1:]]
    inverse = call(
        lambda where, *refs: factor_kernel(where, places, 1.0 / (terms * n_vocab), *refs),
        jax.ShapeDtypeStruct((width, width), f32),
        [pltpu.VMEM((width, width), f32)],
        [where],
        gram_pieces,
    )
    basis, projections = call(
        lambda where, *refs: output_kernel(where, v_places, *refs),
        [
            jax.ShapeDtypeStruct((share, width), f32),
            jax.ShapeDtypeStruct((queries, width), f32),
        ],
        [pltpu.VMEM((queries, width), f32)],
        [where],
        [inverse, own_back, *coords],
        keep=False,
    )
    return basis[None], projections


def solution(mesh):
    return jax.shard_map(
        work,
        mesh=mesh,
        in_specs=(
            P("doc", "vocab", None, None, None),
            P("doc", "vocab", None),
            P("doc", "vocab", None),
            P("doc", "vocab"),
            P("vocab", None),
            P("doc", "vocab", None),
            P("doc", "vocab", None, None),
        ),
        out_specs=(P("vocab", "doc", None), P("doc", None)),
        check_vma=False,
    )
```

```python
import jax
import jax.numpy as jnp
from jax import lax
from jax.experimental import pallas as pl
from jax.experimental.pallas import tpu as pltpu
from jax.sharding import PartitionSpec as P


ROW_TILES = 8
PANEL = 32
AHEAD = 10
TILE = 128
CORES = 2
HALVES = 2

precise = lax.Precision.HIGHEST
smem = pl.BlockSpec(memory_space=pltpu.SMEM)
vmem = pl.BlockSpec(memory_space=pltpu.VMEM)
f32 = jnp.float32
bf16 = jnp.bfloat16


def dot(left, right, dims, precision=None):
    return lax.dot_general(
        left, right, (dims, ((), ())), precision=precision, preferred_element_type=f32
    )


def invert_factor(work, first, last):
    tiles = work.shape[0] // TILE
    chunks = PANEL // 8
    panels = TILE // PANEL
    sub_id = lax.broadcasted_iota(jnp.int32, (8, TILE), 0)
    lane_id = lax.broadcasted_iota(jnp.int32, (8, TILE), 1)
    square_lanes = lax.broadcasted_iota(jnp.int32, (TILE, TILE), 1)

    def block(o, carry):
        base = pl.multiple_of(o * TILE, TILE)

        def earlier(b, inner):
            above_at = pl.multiple_of(b * TILE, TILE)
            left = work[pl.ds(above_at, TILE), pl.ds(base, TILE)]
            update = dot(left, work[pl.ds(above_at, TILE), :], ((0,), (0,)), precise)
            work[pl.ds(base, TILE), :] = work[pl.ds(base, TILE), :] - update
            work[pl.ds(above_at, TILE), pl.ds(base, TILE)] = jnp.zeros((TILE, TILE), f32)
            return inner

        lax.fori_loop(0, o, earlier, 0)
        for s in range(panels):
            lo = s * PANEL
            at = base + lo
            if s > 0:
                left = work[pl.ds(base, TILE), pl.ds(base, TILE)].T[lo : lo + PANEL]
                left = jnp.where(square_lanes[:PANEL] < lo, left, 0.0)
                update = dot(left, work[pl.ds(base, TILE), :], ((1,), (0,)), precise)
                above = work[pl.ds(base, lo), pl.ds(base, TILE)]
                gone = (square_lanes[:lo] >= lo) & (square_lanes[:lo] < lo + PANEL)
                work[pl.ds(base, lo), pl.ds(base, TILE)] = jnp.where(gone, 0.0, above)
            rows = []
            for r in range(chunks):
                line = []
                for t in range(tiles):
                    old = work[pl.ds(at + 8 * r, 8), t * TILE : (t + 1) * TILE]
                    if s > 0:
                        old = jnp.where((lane_id < lo) & (o == t), 0.0, old)
                        old = old - update[8 * r : 8 * r + 8, t * TILE : (t + 1) * TILE]
                    line.append(old)
                rows.append(line)
            own = []
            for r in range(chunks):
                mine = rows[r][0]
                for t in range(1, tiles):
                    mine = jnp.where(o == t, rows[r][t], mine)
                own.append(mine)
            in_panel = (lane_id >= lo) & (lane_id < lo + PANEL)
            for r in range(chunks):
                eye = (lane_id == lo + 8 * r + sub_id).astype(f32)
                for t in range(tiles):
                    rows[r][t] = jnp.where(in_panel & (o == t), eye, rows[r][t])

            def column(l):
                return [
                    jnp.broadcast_to(own[r][:, lo + l : lo + l + 1], (8, TILE)) if r >= l // 8 else None
                    for r in range(chunks)
                ]

            col = {l: column(l) for l in range(AHEAD)}
            for k in range(PANEL):
                kr, ks = k // 8, k % 8
                pivot = jnp.broadcast_to(col[k][kr][ks : ks + 1, :], (8, TILE))
                q = lax.rsqrt(pivot)
                lcol = [col[k][r] * q if r >= kr else None for r in range(chunks)]
                for l in range(k + 1, min(k + AHEAD, PANEL)):
                    e = jnp.broadcast_to(lcol[l // 8][l % 8 : l % 8 + 1, :], (8, TILE))
                    for r in range(l // 8, chunks):
                        col[l][r] = col[l][r] - lcol[r] * e
                if k + AHEAD < PANEL:
                    rk = jnp.broadcast_to(own[kr][ks : ks + 1, :], (8, TILE)) * q
                    for r in range(kr, chunks):
                        own[r] = own[r] - lcol[r] * rk
                    col[k + AHEAD] = column(k + AHEAD)
                below = jnp.where(sub_id > ks, lcol[kr], 0.0)
                for t in range(tiles):
                    rk = jnp.broadcast_to(rows[kr][t][ks : ks + 1, :], (8, TILE)) * q
                    rows[kr][t] = jnp.where(sub_id == ks, rk, rows[kr][t] - below * rk)
                    for r in range(kr + 1, chunks):
                        rows[r][t] = rows[r][t] - lcol[r] * rk
            for r in range(chunks):
                for t in range(tiles):
                    work[pl.ds(at + 8 * r, 8), t * TILE : (t + 1) * TILE] = rows[r][t]
        return carry

    lax.fori_loop(first, last, block, 0)


def dense_kernel(where, halves, places, tiles, *refs):
    outs, dense = refs[:-1], refs[-1]
    rows = dense.shape[0] // len(outs)
    slots = tiles.shape[0]
    dense[...] = jnp.zeros_like(dense)

    def place(s, carry):
        r = pl.multiple_of(where[3 + s] * TILE, TILE)
        c = pl.multiple_of(where[3 + slots + s] * TILE, TILE)
        dense[pl.ds(r, TILE), pl.ds(c, TILE)] = tiles[s]
        return carry

    lax.fori_loop(0, where[2], place, 0)
    for i, out in enumerate(outs):
        block = lax.bitwise_xor(where[0], places[i // halves]) * halves + i % halves
        out[...] = dense[pl.ds(pl.multiple_of(block * rows, rows), rows), :]


def turn_kernel(*refs):
    blocks, out = refs[:-1], refs[-1]
    whole = jnp.concatenate([block[...] for block in blocks], axis=0)
    out[...] = whole.T


def assemble_kernel(where, places, *refs):
    pieces, out = refs[:-1], refs[-1]
    rows = pieces[0].shape[1]
    for piece, place in zip(pieces, places):
        at = pl.multiple_of(lax.bitwise_xor(where[1], place) * rows, rows)
        out[:, pl.ds(at, rows), :] = piece[...]


def forward_kernel(*refs):
    blocks = refs[:-3]
    own_sketch, others, out = refs[-3:]
    total = dot(blocks[0][...], own_sketch[...], ((1,), (0,)))
    for s in range(1, len(blocks)):
        total = total + dot(blocks[s][...], others[s - 1], ((1,), (0,)))
    out[...] = total.astype(bf16)


def backward_kernel(where, places, turned, *refs):
    outs = refs[-2 - len(places) : -2]
    sketched = refs[: -2 - len(places)]
    whole, full = refs[-2:]
    height = sketched[0].shape[0]
    for i, piece in enumerate(sketched):
        whole[i * height : (i + 1) * height, :] = piece[...]
    full[...] = dot(turned[...], whole[...], ((1,), (0,)))
    rows = outs[0].shape[0]
    for out, place in zip(outs, places):
        at = pl.multiple_of(lax.bitwise_xor(where[1], place) * rows, rows)
        out[...] = full[pl.ds(at, rows), :]


def gram_kernel(where, places, *refs):
    pieces = refs[: len(places)]
    gram, back, product = refs[len(places) :]
    rows = pieces[0].shape[0]
    for i, piece in enumerate(pieces):
        back[i * rows : (i + 1) * rows, :] = piece[...]
    width = back.shape[1]
    band = gram.shape[0]
    bands = width // band
    halves = []
    for half, index in enumerate((where[1], bands - 1 - where[1])):
        start = index * band
        tile_at = pl.multiple_of(start // TILE * TILE, TILE)
        product[half] = dot(back[:, pl.ds(tile_at, TILE)], back[...], ((0,), (0,)), precise)
        halves.append(product[half, pl.ds(pl.multiple_of(start - tile_at, band), band), :])
    lead = where[1] * band // PANEL * PANEL
    turned = pltpu.roll(halves[1], lead, 1)
    lanes = lax.broadcasted_iota(jnp.int32, (band, width), 1)
    gram[:, :width] = jnp.where(lanes >= lead, halves[0], turned)
    gram[:, width:] = turned[:, width - TILE :]


def query_dense_kernel(tiles, values, out):
    for c in range(out.shape[1] // TILE):
        total = None
        for j in range(tiles.shape[1]):
            part = jnp.where(tiles[:, j : j + 1] == c, values[:, j * TILE : (j + 1) * TILE], 0.0)
            total = part if total is None else total + part
        out[:, c * TILE : (c + 1) * TILE] = total


def query_kernel(where, places, dense, *refs):
    pieces = refs[: len(places)]
    outs = refs[len(places) : -2]
    back, full = refs[-2:]
    height = pieces[0].shape[0]
    for piece, place in zip(pieces, places):
        at = pl.multiple_of(lax.bitwise_xor(where[1], place) * height, height)
        back[pl.ds(at, height), :] = piece[...]
    full[...] = dot(dense[...], back[...], ((1,), (0,)), precise)
    rows = outs[0].shape[1]
    for place in range(2 * outs[0].shape[0]):
        at = pl.multiple_of(lax.bitwise_xor(where[0], place) * rows, rows)
        outs[place % 2][place // 2] = full[pl.ds(at, rows), :]


def factor_kernel(where, places, scale, *refs):
    pieces, work = refs[: len(places)], refs[-1]
    n = work.shape[0]
    band = pieces[0].shape[0]
    bands = n // band
    lanes = lax.broadcasted_iota(jnp.int32, (band, n), 1)
    for piece, place in zip(pieces, places):
        index = lax.bitwise_xor(where[1], place)
        lead = index * band // PANEL * PANEL
        packed = piece[:, :n] * scale
        tail = piece[:, n:] * scale
        first = jnp.where(lanes >= lead, packed, 0.0)
        work[pl.ds(pl.multiple_of(index * band, band), band), :] = first
        whole = jnp.concatenate([packed[:, : n - TILE], tail], axis=1)
        whole = jnp.where((lanes < lead) | (lanes >= n - PANEL), whole, 0.0)
        second = pltpu.roll(whole, lax.rem(n - lead, n), 1)
        work[pl.ds(pl.multiple_of((bands - 1 - index) * band, band), band), :] = second
    invert_factor(work, 0, n // TILE // 2)


def finish_kernel(begun, work):
    work[...] = begun[...]
    tiles = work.shape[0] // TILE
    invert_factor(work, tiles // 2, tiles)


def output_kernel(where, held_places, *refs):
    inverse, own = refs[0], refs[1]
    coords = refs[2 : 2 + len(held_places)]
    basis, projections, full = refs[2 + len(held_places) :]
    share, rows = own.shape[0], coords[0].shape[1]
    full[:share, :] = own[...]
    for piece, pair in zip(coords, held_places):
        for i, place in enumerate(pair):
            at = pl.multiple_of(lax.bitwise_xor(where[0], place) * rows, rows)
            full[pl.ds(share + at, rows), :] = piece[i]
    product = dot(full[...], inverse[...], ((1,), (1,)), precise)
    basis[...] = product[:share]
    raw = product[share:]
    mean = jnp.sum(raw * raw, axis=1, keepdims=True) * (1.0 / raw.shape[1])
    projections[...] = raw * lax.rsqrt(mean + 1e-06)


def call(kernel, outs, scratch, scalars, arrays, keep=True):
    if keep:
        outs = jax.tree.map(lambda x: pltpu.VMEM(x.shape, x.dtype), outs)
    return pl.pallas_call(
        kernel,
        out_shape=outs,
        in_specs=[smem] * len(scalars) + [vmem] * len(arrays),
        out_specs=jax.tree.map(lambda _: vmem, outs),
        scratch_shapes=scratch,
        compiler_params=pltpu.CompilerParams(vmem_limit_bytes=16 << 20),
    )(*scalars, *[pltpu.with_memory_space_constraint(x, pltpu.VMEM) for x in arrays])


def work(tile_values, tile_rows, tile_columns, counts, sketch, query_tiles, query_values):
    n_doc, n_vocab = lax.axis_size("doc"), lax.axis_size("vocab")
    doc, vocab = lax.axis_index("doc"), lax.axis_index("vocab")
    where = jnp.concatenate(
        [jnp.stack([vocab, doc]).astype(jnp.int32), counts[0], tile_rows[0, 0], tile_columns[0, 0]]
    )
    chips = n_doc // CORES
    edge = tile_values.shape[3]
    terms, width = sketch.shape
    queries = query_tiles.shape[0]
    documents = ROW_TILES * edge
    share = terms // n_doc
    places = [CORES * m + c for m in range(chips) for c in range(CORES)]
    bits = [1 << b for b in reversed(range(n_vocab.bit_length() - 1))]
    v_places = [0]
    for bit in bits:
        v_places += [place | bit for place in v_places]

    def along(x, place):
        return lax.ppermute(x, "vocab", [(a, a ^ place) for a in range(n_vocab)])

    def across(x, place):
        return lax.ppermute(x, "doc", [(a, a ^ place) for a in range(n_doc)])

    def collect(x):
        held = [x]
        for bit in bits:
            near = along(x, bit)
            held += [near] + [along(piece, bit) for piece in held[1:]]
        return held

    def spread(x):
        near = [x]
        for m in range(1, chips):
            near.append(across(x, CORES * m))
        far = [across(piece, 1) for piece in near]
        return [piece for pair in zip(near, far) for piece in pair]

    rows = documents // n_vocab // HALVES
    dense = call(
        lambda where, *refs: dense_kernel(where, HALVES, v_places, *refs),
        [jax.ShapeDtypeStruct((rows, terms), bf16)] * (n_vocab * HALVES),
        [pltpu.VMEM((documents, terms), bf16)],
        [where],
        [tile_values[0, 0]],
    )
    own_terms = lax.dynamic_slice_in_dim(sketch, doc * share, share, 0)
    blocks = [
        [dense[h]] + [along(dense[i * HALVES + h], v_places[i]) for i in range(1, n_vocab)]
        for h in range(HALVES)
    ]
    others = jnp.stack([along(own_terms, place) for place in v_places[1:]])
    term_pieces = spread(others)
    other_sketch = call(
        lambda where, *refs: assemble_kernel(where, places, *refs),
        jax.ShapeDtypeStruct((n_vocab - 1, terms, width), bf16),
        [],
        [where],
        term_pieces,
    )
    turned = call(turn_kernel, jax.ShapeDtypeStruct((terms, documents), bf16), [], [], dense)
    query_dense = call(
        query_dense_kernel,
        jax.ShapeDtypeStruct((queries, terms), f32),
        [],
        [],
        [query_tiles[:, 0], query_values.reshape(queries, -1)],
    )
    gathered = []
    for h in range(HALVES):
        own_sketched = call(
            forward_kernel,
            jax.ShapeDtypeStruct((rows, width), bf16),
            [],
            [],
            [*blocks[h], sketch, other_sketch],
        )
        gathered.append(collect(own_sketched))
    sketched = [gathered[h][i] for i in range(n_vocab) for h in range(HALVES)]
    piece = jax.ShapeDtypeStruct((share, width), f32)
    parted = call(
        lambda where, *refs: backward_kernel(where, places, *refs),
        [piece] * n_doc,
        [pltpu.VMEM((documents, width), bf16), pltpu.VMEM((terms, width), f32)],
        [where],
        [turned, *sketched],
    )
    paired = [parted[CORES * m] + across(parted[CORES * m + 1], 1) for m in range(chips)]
    own_back = paired[0]
    for m in range(1, chips):
        own_back = own_back + across(paired[m], CORES * m)
    back_pieces = spread(own_back)
    band = width // n_doc // 2
    gram_rows = call(
        lambda where, *refs: gram_kernel(where, places, *refs),
        jax.ShapeDtypeStruct((band, width + TILE), f32),
        [pltpu.VMEM((terms, width), f32), pltpu.VMEM((2, TILE, width), f32)],
        [where],
        back_pieces,
    )
    for bit in reversed(bits):
        gram_rows = gram_rows + along(gram_rows, bit)
    query_rows = queries // n_vocab
    even, odd = call(
        lambda where, *refs: query_kernel(where, places, *refs),
        [jax.ShapeDtypeStruct((n_vocab // 2, query_rows, width), f32)] * 2,
        [pltpu.VMEM((terms, width), f32), pltpu.VMEM((queries, width), f32)],
        [where],
        [query_dense, *back_pieces],
    )
    partial_query = even + along(odd, 1)
    gram_pieces = spread(gram_rows)
    bit, top = 2, n_vocab // 2
    while bit < top:
        partial_query = partial_query[0::2] + along(partial_query[1::2], bit)
        bit *= 2
    own_query = partial_query + along(partial_query[::-1], top)
    begun = call(
        lambda where, *refs: factor_kernel(where, places, 1.0 / (terms * n_vocab), *refs),
        jax.ShapeDtypeStruct((width, width), f32),
        [],
        [where],
        gram_pieces,
    )
    coords, held_places = [own_query], [(0, top)]
    for bit in bits[1:]:
        coords += [along(piece, bit) for piece in coords]
        held_places += [(near | bit, far | bit) for near, far in held_places]
    inverse = call(finish_kernel, jax.ShapeDtypeStruct((width, width), f32), [], [], [begun])
    basis, projections = call(
        lambda where, *refs: output_kernel(where, held_places, *refs),
        [
            jax.ShapeDtypeStruct((share, width), f32),
            jax.ShapeDtypeStruct((queries, width), f32),
        ],
        [pltpu.VMEM((share + queries, width), f32)],
        [where],
        [inverse, own_back, *coords],
        keep=False,
    )
    return basis[None], projections


def solution(mesh):
    return jax.shard_map(
        work,
        mesh=mesh,
        in_specs=(
            P("doc", "vocab", None, None, None),
            P("doc", "vocab", None),
            P("doc", "vocab", None),
            P("doc", "vocab"),
            P("vocab", None),
            P("doc", "vocab", None),
            P("doc", "vocab", None, None),
        ),
        out_specs=(P("vocab", "doc", None), P("doc", None)),
        check_vma=False,
    )
```

```python
import jax
import jax.numpy as jnp
from jax import lax
from jax.experimental import pallas as pl
from jax.experimental.pallas import tpu as pltpu
from jax.sharding import PartitionSpec as P


ROW_TILES = 8
PANEL = 32
AHEAD = 10
TILE = 128
CORES = 2
HALVES = 2

precise = lax.Precision.HIGHEST
smem = pl.BlockSpec(memory_space=pltpu.SMEM)
vmem = pl.BlockSpec(memory_space=pltpu.VMEM)
f32 = jnp.float32
bf16 = jnp.bfloat16


def dot(left, right, dims, precision=None):
    return lax.dot_general(
        left, right, (dims, ((), ())), precision=precision, preferred_element_type=f32
    )


def invert_factor(work, first, last):
    tiles = work.shape[0] // TILE
    chunks = PANEL // 8
    panels = TILE // PANEL
    sub_id = lax.broadcasted_iota(jnp.int32, (8, TILE), 0)
    lane_id = lax.broadcasted_iota(jnp.int32, (8, TILE), 1)
    square_lanes = lax.broadcasted_iota(jnp.int32, (TILE, TILE), 1)

    def block(o, carry):
        base = pl.multiple_of(o * TILE, TILE)

        def earlier(b, inner):
            above_at = pl.multiple_of(b * TILE, TILE)
            left = work[pl.ds(above_at, TILE), pl.ds(base, TILE)]
            update = dot(left, work[pl.ds(above_at, TILE), :], ((0,), (0,)), precise)
            work[pl.ds(base, TILE), :] = work[pl.ds(base, TILE), :] - update
            work[pl.ds(above_at, TILE), pl.ds(base, TILE)] = jnp.zeros((TILE, TILE), f32)
            return inner

        lax.fori_loop(0, o, earlier, 0)
        for s in range(panels):
            lo = s * PANEL
            at = base + lo
            if s > 0:
                left = work[pl.ds(base, TILE), pl.ds(base, TILE)].T[lo : lo + PANEL]
                left = jnp.where(square_lanes[:PANEL] < lo, left, 0.0)
                update = dot(left, work[pl.ds(base, TILE), :], ((1,), (0,)), precise)
                above = work[pl.ds(base, lo), pl.ds(base, TILE)]
                gone = (square_lanes[:lo] >= lo) & (square_lanes[:lo] < lo + PANEL)
                work[pl.ds(base, lo), pl.ds(base, TILE)] = jnp.where(gone, 0.0, above)
            rows = []
            for r in range(chunks):
                line = []
                for t in range(tiles):
                    old = work[pl.ds(at + 8 * r, 8), t * TILE : (t + 1) * TILE]
                    if s > 0:
                        old = jnp.where((lane_id < lo) & (o == t), 0.0, old)
                        old = old - update[8 * r : 8 * r + 8, t * TILE : (t + 1) * TILE]
                    line.append(old)
                rows.append(line)
            own = []
            for r in range(chunks):
                mine = rows[r][0]
                for t in range(1, tiles):
                    mine = jnp.where(o == t, rows[r][t], mine)
                own.append(mine)
            in_panel = (lane_id >= lo) & (lane_id < lo + PANEL)
            for r in range(chunks):
                eye = (lane_id == lo + 8 * r + sub_id).astype(f32)
                for t in range(tiles):
                    rows[r][t] = jnp.where(in_panel & (o == t), eye, rows[r][t])

            def column(l):
                return [
                    jnp.broadcast_to(own[r][:, lo + l : lo + l + 1], (8, TILE)) if r >= l // 8 else None
                    for r in range(chunks)
                ]

            col = {l: column(l) for l in range(AHEAD)}
            for k in range(PANEL):
                kr, ks = k // 8, k % 8
                pivot = jnp.broadcast_to(col[k][kr][ks : ks + 1, :], (8, TILE))
                q = lax.rsqrt(pivot)
                lcol = [col[k][r] * q if r >= kr else None for r in range(chunks)]
                for l in range(k + 1, min(k + AHEAD, PANEL)):
                    e = jnp.broadcast_to(lcol[l // 8][l % 8 : l % 8 + 1, :], (8, TILE))
                    for r in range(l // 8, chunks):
                        col[l][r] = col[l][r] - lcol[r] * e
                if k + AHEAD < PANEL:
                    rk = jnp.broadcast_to(own[kr][ks : ks + 1, :], (8, TILE)) * q
                    for r in range(kr, chunks):
                        own[r] = own[r] - lcol[r] * rk
                    col[k + AHEAD] = column(k + AHEAD)
                below = jnp.where(sub_id > ks, lcol[kr], 0.0)
                for t in range(tiles):
                    rk = jnp.broadcast_to(rows[kr][t][ks : ks + 1, :], (8, TILE)) * q
                    rows[kr][t] = jnp.where(sub_id == ks, rk, rows[kr][t] - below * rk)
                    for r in range(kr + 1, chunks):
                        rows[r][t] = rows[r][t] - lcol[r] * rk
            for r in range(chunks):
                for t in range(tiles):
                    work[pl.ds(at + 8 * r, 8), t * TILE : (t + 1) * TILE] = rows[r][t]
        return carry

    lax.fori_loop(first, last, block, 0)


def dense_kernel(where, halves, places, tiles, *refs):
    outs, dense = refs[:-1], refs[-1]
    rows = dense.shape[0] // len(outs)
    slots = tiles.shape[0]
    dense[...] = jnp.zeros_like(dense)

    def place(s, carry):
        r = pl.multiple_of(where[3 + s] * TILE, TILE)
        c = pl.multiple_of(where[3 + slots + s] * TILE, TILE)
        dense[pl.ds(r, TILE), pl.ds(c, TILE)] = tiles[s]
        return carry

    lax.fori_loop(0, where[2], place, 0)
    for i, out in enumerate(outs):
        block = lax.bitwise_xor(where[0], places[i // halves]) * halves + i % halves
        out[...] = dense[pl.ds(pl.multiple_of(block * rows, rows), rows), :]


def turn_kernel(*refs):
    blocks, out = refs[:-1], refs[-1]
    whole = jnp.concatenate([block[...] for block in blocks], axis=0)
    out[...] = whole.T


def assemble_kernel(where, places, *refs):
    pieces, out = refs[:-1], refs[-1]
    rows = pieces[0].shape[1]
    for piece, place in zip(pieces, places):
        at = pl.multiple_of(lax.bitwise_xor(where[1], place) * rows, rows)
        out[:, pl.ds(at, rows), :] = piece[...]


def forward_kernel(*refs):
    blocks = refs[:-3]
    own_sketch, others, out = refs[-3:]
    total = dot(blocks[0][...], own_sketch[...], ((1,), (0,)))
    for s in range(1, len(blocks)):
        total = total + dot(blocks[s][...], others[s - 1], ((1,), (0,)))
    out[...] = total.astype(bf16)


def backward_kernel(where, places, turned, *refs):
    outs = refs[-2 - len(places) : -2]
    sketched = refs[: -2 - len(places)]
    whole, full = refs[-2:]
    height = sketched[0].shape[0]
    for i, piece in enumerate(sketched):
        whole[i * height : (i + 1) * height, :] = piece[...]
    full[...] = dot(turned[...], whole[...], ((1,), (0,)))
    rows = outs[0].shape[0]
    for out, place in zip(outs, places):
        at = pl.multiple_of(lax.bitwise_xor(where[1], place) * rows, rows)
        out[...] = full[pl.ds(at, rows), :]


def gram_kernel(where, places, *refs):
    pieces = refs[: len(places)]
    gram, back, product = refs[len(places) :]
    rows = pieces[0].shape[0]
    for i, piece in enumerate(pieces):
        back[i * rows : (i + 1) * rows, :] = piece[...]
    width = back.shape[1]
    band = gram.shape[0]
    bands = width // band
    halves = []
    for half, index in enumerate((where[1], bands - 1 - where[1])):
        start = index * band
        tile_at = pl.multiple_of(start // TILE * TILE, TILE)
        product[half] = dot(back[:, pl.ds(tile_at, TILE)], back[...], ((0,), (0,)), precise)
        halves.append(product[half, pl.ds(pl.multiple_of(start - tile_at, band), band), :])
    lead = where[1] * band // PANEL * PANEL
    turned = pltpu.roll(halves[1], lead, 1)
    lanes = lax.broadcasted_iota(jnp.int32, (band, width), 1)
    gram[:, :width] = jnp.where(lanes >= lead, halves[0], turned)
    gram[:, width:] = turned[:, width - TILE :]


def query_dense_kernel(tiles, values, out):
    for c in range(out.shape[1] // TILE):
        total = None
        for j in range(tiles.shape[1]):
            part = jnp.where(tiles[:, j : j + 1] == c, values[:, j * TILE : (j + 1) * TILE], 0.0)
            total = part if total is None else total + part
        out[:, c * TILE : (c + 1) * TILE] = total


def query_kernel(where, places, dense, *refs):
    pieces = refs[: len(places)]
    outs = refs[len(places) : -2]
    back, full = refs[-2:]
    height = pieces[0].shape[0]
    for piece, place in zip(pieces, places):
        at = pl.multiple_of(lax.bitwise_xor(where[1], place) * height, height)
        back[pl.ds(at, height), :] = piece[...]
    full[...] = dot(dense[...], back[...], ((1,), (0,)), precise)
    rows = outs[0].shape[1]
    for place in range(2 * outs[0].shape[0]):
        at = pl.multiple_of(lax.bitwise_xor(where[0], place) * rows, rows)
        outs[place % 2][place // 2] = full[pl.ds(at, rows), :]


def factor_kernel(where, places, scale, *refs):
    pieces, work = refs[: len(places)], refs[-1]
    n = work.shape[0]
    band = pieces[0].shape[0]
    bands = n // band
    lanes = lax.broadcasted_iota(jnp.int32, (band, n), 1)
    for piece, place in zip(pieces, places):
        index = lax.bitwise_xor(where[1], place)
        lead = index * band // PANEL * PANEL
        packed = piece[:, :n] * scale
        tail = piece[:, n:] * scale
        first = jnp.where(lanes >= lead, packed, 0.0)
        work[pl.ds(pl.multiple_of(index * band, band), band), :] = first
        whole = jnp.concatenate([packed[:, : n - TILE], tail], axis=1)
        whole = jnp.where((lanes < lead) | (lanes >= n - PANEL), whole, 0.0)
        second = pltpu.roll(whole, lax.rem(n - lead, n), 1)
        work[pl.ds(pl.multiple_of((bands - 1 - index) * band, band), band), :] = second
    invert_factor(work, 0, n // TILE // 2)


def finish_kernel(begun, work):
    work[...] = begun[...]
    tiles = work.shape[0] // TILE
    invert_factor(work, tiles // 2, tiles)


def output_kernel(where, held_places, *refs):
    inverse, own = refs[0], refs[1]
    coords = refs[2 : 2 + len(held_places)]
    basis, projections, full = refs[2 + len(held_places) :]
    share, rows = own.shape[0], coords[0].shape[1]
    full[:share, :] = own[...]
    for piece, pair in zip(coords, held_places):
        for i, place in enumerate(pair):
            at = pl.multiple_of(lax.bitwise_xor(where[0], place) * rows, rows)
            full[pl.ds(share + at, rows), :] = piece[i]
    product = dot(full[...], inverse[...], ((1,), (1,)), precise)
    basis[...] = product[:share]
    raw = product[share:]
    mean = jnp.sum(raw * raw, axis=1, keepdims=True) * (1.0 / raw.shape[1])
    projections[...] = raw * lax.rsqrt(mean + 1e-06)


def call(kernel, outs, scratch, scalars, arrays, keep=True):
    if keep:
        outs = jax.tree.map(lambda x: pltpu.VMEM(x.shape, x.dtype), outs)
    return pl.pallas_call(
        kernel,
        out_shape=outs,
        in_specs=[smem] * len(scalars) + [vmem] * len(arrays),
        out_specs=jax.tree.map(lambda _: vmem, outs),
        scratch_shapes=scratch,
        compiler_params=pltpu.CompilerParams(vmem_limit_bytes=16 << 20),
    )(*scalars, *[pltpu.with_memory_space_constraint(x, pltpu.VMEM) for x in arrays])


def work(tile_values, tile_rows, tile_columns, counts, sketch, query_tiles, query_values):
    n_doc, n_vocab = lax.axis_size("doc"), lax.axis_size("vocab")
    doc, vocab = lax.axis_index("doc"), lax.axis_index("vocab")
    where = jnp.concatenate(
        [jnp.stack([vocab, doc]).astype(jnp.int32), counts[0], tile_rows[0, 0], tile_columns[0, 0]]
    )
    chips = n_doc // CORES
    edge = tile_values.shape[3]
    terms, width = sketch.shape
    queries = query_tiles.shape[0]
    documents = ROW_TILES * edge
    share = terms // n_doc
    places = [CORES * m + c for m in range(chips) for c in range(CORES)]
    bits = [1 << b for b in reversed(range(n_vocab.bit_length() - 1))]
    v_places = [0]
    for bit in bits:
        v_places += [place | bit for place in v_places]

    def along(x, place):
        return lax.ppermute(x, "vocab", [(a, a ^ place) for a in range(n_vocab)])

    def across(x, place):
        return lax.ppermute(x, "doc", [(a, a ^ place) for a in range(n_doc)])

    def collect(x):
        held = [x]
        for bit in bits:
            near = along(x, bit)
            held += [near] + [along(piece, bit) for piece in held[1:]]
        return held

    def spread(x):
        near = [x]
        for m in range(1, chips):
            near.append(across(x, CORES * m))
        far = [across(piece, 1) for piece in near]
        return [piece for pair in zip(near, far) for piece in pair]

    rows = documents // n_vocab // HALVES
    dense = call(
        lambda where, *refs: dense_kernel(where, HALVES, v_places, *refs),
        [jax.ShapeDtypeStruct((rows, terms), bf16)] * (n_vocab * HALVES),
        [pltpu.VMEM((documents, terms), bf16)],
        [where],
        [tile_values[0, 0]],
    )
    own_terms = lax.dynamic_slice_in_dim(sketch, doc * share, share, 0)
    blocks = []
    for h in range(HALVES):
        moved = [along(dense[i * HALVES + h], v_places[i]) for i in range(1, n_vocab)]
        blocks.append([dense[h]] + moved)
    others = jnp.stack([along(own_terms, place) for place in v_places[1:]])
    term_pieces = spread(others)
    other_sketch = call(
        lambda where, *refs: assemble_kernel(where, places, *refs),
        jax.ShapeDtypeStruct((n_vocab - 1, terms, width), bf16),
        [],
        [where],
        term_pieces,
    )
    turned = call(turn_kernel, jax.ShapeDtypeStruct((terms, documents), bf16), [], [], dense)
    query_dense = call(
        query_dense_kernel,
        jax.ShapeDtypeStruct((queries, terms), f32),
        [],
        [],
        [query_tiles[:, 0], query_values.reshape(queries, -1)],
    )
    gathered = []
    for h in range(HALVES):
        own_sketched = call(
            forward_kernel,
            jax.ShapeDtypeStruct((rows, width), bf16),
            [],
            [],
            [*blocks[h], sketch, other_sketch],
        )
        gathered.append(collect(own_sketched))
    sketched = [gathered[h][i] for i in range(n_vocab) for h in range(HALVES)]
    piece = jax.ShapeDtypeStruct((share, width), f32)
    parted = call(
        lambda where, *refs: backward_kernel(where, places, *refs),
        [piece] * n_doc,
        [pltpu.VMEM((documents, width), bf16), pltpu.VMEM((terms, width), f32)],
        [where],
        [turned, *sketched],
    )
    paired = [parted[CORES * m] + across(parted[CORES * m + 1], 1) for m in range(chips)]
    own_back = paired[0]
    for m in range(1, chips):
        own_back = own_back + across(paired[m], CORES * m)
    back_pieces = spread(own_back)
    band = width // n_doc // 2
    gram_rows = call(
        lambda where, *refs: gram_kernel(where, places, *refs),
        jax.ShapeDtypeStruct((band, width + TILE), f32),
        [pltpu.VMEM((terms, width), f32), pltpu.VMEM((2, TILE, width), f32)],
        [where],
        back_pieces,
    )
    for bit in reversed(bits):
        gram_rows = gram_rows + along(gram_rows, bit)
    query_rows = queries // n_vocab
    even, odd = call(
        lambda where, *refs: query_kernel(where, places, *refs),
        [jax.ShapeDtypeStruct((n_vocab // 2, query_rows, width), f32)] * 2,
        [pltpu.VMEM((terms, width), f32), pltpu.VMEM((queries, width), f32)],
        [where],
        [query_dense, *back_pieces],
    )
    partial_query = even + along(odd, 1)
    gram_pieces = spread(gram_rows)
    bit, top = 2, n_vocab // 2
    while bit < top:
        partial_query = partial_query[0::2] + along(partial_query[1::2], bit)
        bit *= 2
    own_query = partial_query + along(partial_query[::-1], top)
    begun = call(
        lambda where, *refs: factor_kernel(where, places, 1.0 / (terms * n_vocab), *refs),
        jax.ShapeDtypeStruct((width, width), f32),
        [],
        [where],
        gram_pieces,
    )
    coords, held_places = [own_query], [(0, top)]
    for bit in bits[1:]:
        coords += [along(piece, bit) for piece in coords]
        held_places += [(near | bit, far | bit) for near, far in held_places]
    inverse = call(finish_kernel, jax.ShapeDtypeStruct((width, width), f32), [], [], [begun])
    basis, projections = call(
        lambda where, *refs: output_kernel(where, held_places, *refs),
        [
            jax.ShapeDtypeStruct((share, width), f32),
            jax.ShapeDtypeStruct((queries, width), f32),
        ],
        [pltpu.VMEM((share + queries, width), f32)],
        [where],
        [inverse, own_back, *coords],
        keep=False,
    )
    return basis[None], projections


def solution(mesh):
    return jax.shard_map(
        work,
        mesh=mesh,
        in_specs=(
            P("doc", "vocab", None, None, None),
            P("doc", "vocab", None),
            P("doc", "vocab", None),
            P("doc", "vocab"),
            P("vocab", None),
            P("doc", "vocab", None),
            P("doc", "vocab", None, None),
        ),
        out_specs=(P("vocab", "doc", None), P("doc", None)),
        check_vma=False,
    )
```

```python
import jax
import jax.numpy as jnp
from jax import lax
from jax.experimental import pallas as pl
from jax.experimental.pallas import tpu as pltpu
from jax.sharding import PartitionSpec as P


ROW_TILES = 8
PANEL = 32
AHEAD = 10
TILE = 128
CORES = 2
HALVES = 2

precise = lax.Precision.HIGHEST
smem = pl.BlockSpec(memory_space=pltpu.SMEM)
vmem = pl.BlockSpec(memory_space=pltpu.VMEM)
f32 = jnp.float32
bf16 = jnp.bfloat16


def dot(left, right, dims, precision=None):
    return lax.dot_general(
        left, right, (dims, ((), ())), precision=precision, preferred_element_type=f32
    )


def invert_factor(work, first, last):
    tiles = work.shape[0] // TILE
    chunks = PANEL // 8
    panels = TILE // PANEL
    sub_id = lax.broadcasted_iota(jnp.int32, (8, TILE), 0)
    lane_id = lax.broadcasted_iota(jnp.int32, (8, TILE), 1)
    square_lanes = lax.broadcasted_iota(jnp.int32, (TILE, TILE), 1)

    def block(o, carry):
        base = pl.multiple_of(o * TILE, TILE)

        def earlier(b, inner):
            above_at = pl.multiple_of(b * TILE, TILE)
            left = work[pl.ds(above_at, TILE), pl.ds(base, TILE)]
            update = dot(left, work[pl.ds(above_at, TILE), :], ((0,), (0,)), precise)
            work[pl.ds(base, TILE), :] = work[pl.ds(base, TILE), :] - update
            work[pl.ds(above_at, TILE), pl.ds(base, TILE)] = jnp.zeros((TILE, TILE), f32)
            return inner

        lax.fori_loop(0, o, earlier, 0)
        for s in range(panels):
            lo = s * PANEL
            at = base + lo
            if s > 0:
                left = work[pl.ds(base, TILE), pl.ds(base, TILE)].T[lo : lo + PANEL]
                left = jnp.where(square_lanes[:PANEL] < lo, left, 0.0)
                update = dot(left, work[pl.ds(base, TILE), :], ((1,), (0,)), precise)
                above = work[pl.ds(base, lo), pl.ds(base, TILE)]
                gone = (square_lanes[:lo] >= lo) & (square_lanes[:lo] < lo + PANEL)
                work[pl.ds(base, lo), pl.ds(base, TILE)] = jnp.where(gone, 0.0, above)
            rows = []
            for r in range(chunks):
                line = []
                for t in range(tiles):
                    old = work[pl.ds(at + 8 * r, 8), t * TILE : (t + 1) * TILE]
                    if s > 0:
                        old = jnp.where((lane_id < lo) & (o == t), 0.0, old)
                        old = old - update[8 * r : 8 * r + 8, t * TILE : (t + 1) * TILE]
                    line.append(old)
                rows.append(line)
            own = []
            for r in range(chunks):
                mine = rows[r][0]
                for t in range(1, tiles):
                    mine = jnp.where(o == t, rows[r][t], mine)
                own.append(mine)
            in_panel = (lane_id >= lo) & (lane_id < lo + PANEL)
            for r in range(chunks):
                eye = (lane_id == lo + 8 * r + sub_id).astype(f32)
                for t in range(tiles):
                    rows[r][t] = jnp.where(in_panel & (o == t), eye, rows[r][t])

            def column(l):
                return [
                    jnp.broadcast_to(own[r][:, lo + l : lo + l + 1], (8, TILE)) if r >= l // 8 else None
                    for r in range(chunks)
                ]

            col = {l: column(l) for l in range(AHEAD)}
            for k in range(PANEL):
                kr, ks = k // 8, k % 8
                pivot = jnp.broadcast_to(col[k][kr][ks : ks + 1, :], (8, TILE))
                q = lax.rsqrt(pivot)
                lcol = [col[k][r] * q if r >= kr else None for r in range(chunks)]
                for l in range(k + 1, min(k + AHEAD, PANEL)):
                    e = jnp.broadcast_to(lcol[l // 8][l % 8 : l % 8 + 1, :], (8, TILE))
                    for r in range(l // 8, chunks):
                        col[l][r] = col[l][r] - lcol[r] * e
                if k + AHEAD < PANEL:
                    rk = jnp.broadcast_to(own[kr][ks : ks + 1, :], (8, TILE)) * q
                    for r in range(kr, chunks):
                        own[r] = own[r] - lcol[r] * rk
                    col[k + AHEAD] = column(k + AHEAD)
                below = jnp.where(sub_id > ks, lcol[kr], 0.0)
                for t in range(tiles):
                    rk = jnp.broadcast_to(rows[kr][t][ks : ks + 1, :], (8, TILE)) * q
                    rows[kr][t] = jnp.where(sub_id == ks, rk, rows[kr][t] - below * rk)
                    for r in range(kr + 1, chunks):
                        rows[r][t] = rows[r][t] - lcol[r] * rk
            for r in range(chunks):
                for t in range(tiles):
                    work[pl.ds(at + 8 * r, 8), t * TILE : (t + 1) * TILE] = rows[r][t]
        return carry

    lax.fori_loop(first, last, block, 0)


def dense_kernel(where, halves, places, tiles, *refs):
    outs, dense = refs[:-1], refs[-1]
    rows = dense.shape[0] // len(outs)
    slots = tiles.shape[0]
    dense[...] = jnp.zeros_like(dense)

    def place(s, carry):
        r = pl.multiple_of(where[3 + s] * TILE, TILE)
        c = pl.multiple_of(where[3 + slots + s] * TILE, TILE)
        dense[pl.ds(r, TILE), pl.ds(c, TILE)] = tiles[s]
        return carry

    lax.fori_loop(0, where[2], place, 0)
    for i, out in enumerate(outs):
        block = lax.bitwise_xor(where[0], places[i // halves]) * halves + i % halves
        out[...] = dense[pl.ds(pl.multiple_of(block * rows, rows), rows), :]


def turn_kernel(*refs):
    blocks, out = refs[:-1], refs[-1]
    whole = jnp.concatenate([block[...] for block in blocks], axis=0)
    out[...] = whole.T


def assemble_kernel(where, places, *refs):
    pieces, out = refs[:-1], refs[-1]
    rows = pieces[0].shape[1]
    for piece, place in zip(pieces, places):
        at = pl.multiple_of(lax.bitwise_xor(where[1], place) * rows, rows)
        out[:, pl.ds(at, rows), :] = piece[...]


def forward_kernel(*refs):
    blocks = refs[:-3]
    own_sketch, others, out = refs[-3:]
    total = dot(blocks[0][...], own_sketch[...], ((1,), (0,)))
    for s in range(1, len(blocks)):
        total = total + dot(blocks[s][...], others[s - 1], ((1,), (0,)))
    out[...] = total.astype(bf16)


def backward_kernel(where, places, turned, *refs):
    outs = refs[-2 - len(places) : -2]
    sketched = refs[: -2 - len(places)]
    whole, full = refs[-2:]
    height = sketched[0].shape[0]
    for i, piece in enumerate(sketched):
        whole[i * height : (i + 1) * height, :] = piece[...]
    full[...] = dot(turned[...], whole[...], ((1,), (0,)))
    rows = outs[0].shape[0]
    for out, place in zip(outs, places):
        at = pl.multiple_of(lax.bitwise_xor(where[1], place) * rows, rows)
        out[...] = full[pl.ds(at, rows), :]


def gram_kernel(where, places, *refs):
    pieces = refs[: len(places)]
    gram, back = refs[len(places) :]
    rows = pieces[0].shape[0]
    for i, piece in enumerate(pieces):
        back[i * rows : (i + 1) * rows, :] = piece[...]
    width = back.shape[1]
    band = gram.shape[0]
    bands = width // band
    tile_lanes = lax.broadcasted_iota(jnp.int32, (back.shape[0], TILE), 1)
    sides = []
    for half, index in enumerate((where[1], bands - 1 - where[1])):
        start = index * band
        tile_at = pl.multiple_of(start // TILE * TILE, TILE)
        shift = lax.rem(TILE + half * band - (start - tile_at), TILE)
        sides.append(pltpu.roll(back[:, pl.ds(tile_at, TILE)], shift, 1))
    left = jnp.where(tile_lanes < band, sides[0], sides[1])
    product = dot(left, back[...], ((0,), (0,)), precise)
    halves = [product[:band], product[band : 2 * band]]
    lead = where[1] * band // PANEL * PANEL
    turned = pltpu.roll(halves[1], lead, 1)
    lanes = lax.broadcasted_iota(jnp.int32, (band, width), 1)
    gram[:, :width] = jnp.where(lanes >= lead, halves[0], turned)
    gram[:, width:] = turned[:, width - TILE :]


def query_dense_kernel(tiles, values, out):
    for c in range(out.shape[1] // TILE):
        total = None
        for j in range(tiles.shape[1]):
            part = jnp.where(tiles[:, j : j + 1] == c, values[:, j * TILE : (j + 1) * TILE], 0.0)
            total = part if total is None else total + part
        out[:, c * TILE : (c + 1) * TILE] = total


def query_kernel(where, places, dense, *refs):
    pieces = refs[: len(places)]
    outs = refs[len(places) : -2]
    back, full = refs[-2:]
    height = pieces[0].shape[0]
    for piece, place in zip(pieces, places):
        at = pl.multiple_of(lax.bitwise_xor(where[1], place) * height, height)
        back[pl.ds(at, height), :] = piece[...]
    full[...] = dot(dense[...], back[...], ((1,), (0,)), precise)
    rows = outs[0].shape[1]
    for place in range(2 * outs[0].shape[0]):
        at = pl.multiple_of(lax.bitwise_xor(where[0], place) * rows, rows)
        outs[place % 2][place // 2] = full[pl.ds(at, rows), :]


def factor_kernel(where, places, scale, *refs):
    pieces, work = refs[: len(places)], refs[-1]
    n = work.shape[0]
    band = pieces[0].shape[0]
    bands = n // band
    lanes = lax.broadcasted_iota(jnp.int32, (band, n), 1)
    for piece, place in zip(pieces, places):
        index = lax.bitwise_xor(where[1], place)
        lead = index * band // PANEL * PANEL
        packed = piece[:, :n] * scale
        tail = piece[:, n:] * scale
        first = jnp.where(lanes >= lead, packed, 0.0)
        work[pl.ds(pl.multiple_of(index * band, band), band), :] = first
        whole = jnp.concatenate([packed[:, : n - TILE], tail], axis=1)
        whole = jnp.where((lanes < lead) | (lanes >= n - PANEL), whole, 0.0)
        second = pltpu.roll(whole, lax.rem(n - lead, n), 1)
        work[pl.ds(pl.multiple_of((bands - 1 - index) * band, band), band), :] = second
    invert_factor(work, 0, n // TILE // 2)


def finish_kernel(begun, work):
    work[...] = begun[...]
    tiles = work.shape[0] // TILE
    invert_factor(work, tiles // 2, tiles)


def output_kernel(where, held_places, *refs):
    inverse, own = refs[0], refs[1]
    coords = refs[2 : 2 + len(held_places)]
    basis, projections, full = refs[2 + len(held_places) :]
    share, rows = own.shape[0], coords[0].shape[1]
    full[:share, :] = own[...]
    for piece, pair in zip(coords, held_places):
        for i, place in enumerate(pair):
            at = pl.multiple_of(lax.bitwise_xor(where[0], place) * rows, rows)
            full[pl.ds(share + at, rows), :] = piece[i]
    product = dot(full[...], inverse[...], ((1,), (1,)), precise)
    basis[...] = product[:share]
    raw = product[share:]
    mean = jnp.sum(raw * raw, axis=1, keepdims=True) * (1.0 / raw.shape[1])
    projections[...] = raw * lax.rsqrt(mean + 1e-06)


def call(kernel, outs, scratch, scalars, arrays, keep=True):
    if keep:
        outs = jax.tree.map(lambda x: pltpu.VMEM(x.shape, x.dtype), outs)
    return pl.pallas_call(
        kernel,
        out_shape=outs,
        in_specs=[smem] * len(scalars) + [vmem] * len(arrays),
        out_specs=jax.tree.map(lambda _: vmem, outs),
        scratch_shapes=scratch,
        compiler_params=pltpu.CompilerParams(vmem_limit_bytes=16 << 20),
    )(*scalars, *[pltpu.with_memory_space_constraint(x, pltpu.VMEM) for x in arrays])


def work(tile_values, tile_rows, tile_columns, counts, sketch, query_tiles, query_values):
    n_doc, n_vocab = lax.axis_size("doc"), lax.axis_size("vocab")
    doc, vocab = lax.axis_index("doc"), lax.axis_index("vocab")
    where = jnp.concatenate(
        [jnp.stack([vocab, doc]).astype(jnp.int32), counts[0], tile_rows[0, 0], tile_columns[0, 0]]
    )
    chips = n_doc // CORES
    edge = tile_values.shape[3]
    terms, width = sketch.shape
    queries = query_tiles.shape[0]
    documents = ROW_TILES * edge
    share = terms // n_doc
    places = [CORES * m + c for m in range(chips) for c in range(CORES)]
    bits = [1 << b for b in reversed(range(n_vocab.bit_length() - 1))]
    v_places = [0]
    for bit in bits:
        v_places += [place | bit for place in v_places]

    def along(x, place):
        return lax.ppermute(x, "vocab", [(a, a ^ place) for a in range(n_vocab)])

    def across(x, place):
        return lax.ppermute(x, "doc", [(a, a ^ place) for a in range(n_doc)])

    def collect(x):
        held = [x]
        for bit in bits:
            near = along(x, bit)
            held += [near] + [along(piece, bit) for piece in held[1:]]
        return held

    def spread(x):
        near = [x]
        for m in range(1, chips):
            near.append(across(x, CORES * m))
        far = [across(piece, 1) for piece in near]
        return [piece for pair in zip(near, far) for piece in pair]

    rows = documents // n_vocab // HALVES
    dense = call(
        lambda where, *refs: dense_kernel(where, HALVES, v_places, *refs),
        [jax.ShapeDtypeStruct((rows, terms), bf16)] * (n_vocab * HALVES),
        [pltpu.VMEM((documents, terms), bf16)],
        [where],
        [tile_values[0, 0]],
    )
    own_terms = lax.dynamic_slice_in_dim(sketch, doc * share, share, 0)
    blocks = []
    for h in range(HALVES):
        moved = [along(dense[i * HALVES + h], v_places[i]) for i in range(1, n_vocab)]
        blocks.append([dense[h]] + moved)
    others = jnp.stack([along(own_terms, place) for place in v_places[1:]])
    term_pieces = spread(others)
    other_sketch = call(
        lambda where, *refs: assemble_kernel(where, places, *refs),
        jax.ShapeDtypeStruct((n_vocab - 1, terms, width), bf16),
        [],
        [where],
        term_pieces,
    )
    turned = call(turn_kernel, jax.ShapeDtypeStruct((terms, documents), bf16), [], [], dense)
    query_dense = call(
        query_dense_kernel,
        jax.ShapeDtypeStruct((queries, terms), f32),
        [],
        [],
        [query_tiles[:, 0], query_values.reshape(queries, -1)],
    )
    gathered = []
    for h in range(HALVES):
        own_sketched = call(
            forward_kernel,
            jax.ShapeDtypeStruct((rows, width), bf16),
            [],
            [],
            [*blocks[h], sketch, other_sketch],
        )
        gathered.append(collect(own_sketched))
    sketched = [gathered[h][i] for i in range(n_vocab) for h in range(HALVES)]
    piece = jax.ShapeDtypeStruct((share, width), f32)
    parted = call(
        lambda where, *refs: backward_kernel(where, places, *refs),
        [piece] * n_doc,
        [pltpu.VMEM((documents, width), bf16), pltpu.VMEM((terms, width), f32)],
        [where],
        [turned, *sketched],
    )
    paired = [parted[CORES * m] + across(parted[CORES * m + 1], 1) for m in range(chips)]
    own_back = paired[0]
    for m in range(1, chips):
        own_back = own_back + across(paired[m], CORES * m)
    back_pieces = spread(own_back)
    band = width // n_doc // 2
    gram_rows = call(
        lambda where, *refs: gram_kernel(where, places, *refs),
        jax.ShapeDtypeStruct((band, width + TILE), f32),
        [pltpu.VMEM((terms, width), f32)],
        [where],
        back_pieces,
    )
    for bit in reversed(bits):
        gram_rows = gram_rows + along(gram_rows, bit)
    query_rows = queries // n_vocab
    even, odd = call(
        lambda where, *refs: query_kernel(where, places, *refs),
        [jax.ShapeDtypeStruct((n_vocab // 2, query_rows, width), f32)] * 2,
        [pltpu.VMEM((terms, width), f32), pltpu.VMEM((queries, width), f32)],
        [where],
        [query_dense, *back_pieces],
    )
    partial_query = even + along(odd, 1)
    gram_pieces = spread(gram_rows)
    bit, top = 2, n_vocab // 2
    while bit < top:
        partial_query = partial_query[0::2] + along(partial_query[1::2], bit)
        bit *= 2
    own_query = partial_query + along(partial_query[::-1], top)
    begun = call(
        lambda where, *refs: factor_kernel(where, places, 1.0 / (terms * n_vocab), *refs),
        jax.ShapeDtypeStruct((width, width), f32),
        [],
        [where],
        gram_pieces,
    )
    coords, held_places = [own_query], [(0, top)]
    for bit in bits[1:]:
        coords += [along(piece, bit) for piece in coords]
        held_places += [(near | bit, far | bit) for near, far in held_places]
    inverse = call(finish_kernel, jax.ShapeDtypeStruct((width, width), f32), [], [], [begun])
    basis, projections = call(
        lambda where, *refs: output_kernel(where, held_places, *refs),
        [
            jax.ShapeDtypeStruct((share, width), f32),
            jax.ShapeDtypeStruct((queries, width), f32),
        ],
        [pltpu.VMEM((share + queries, width), f32)],
        [where],
        [inverse, own_back, *coords],
        keep=False,
    )
    return basis[None], projections


def solution(mesh):
    return jax.shard_map(
        work,
        mesh=mesh,
        in_specs=(
            P("doc", "vocab", None, None, None),
            P("doc", "vocab", None),
            P("doc", "vocab", None),
            P("doc", "vocab"),
            P("vocab", None),
            P("doc", "vocab", None),
            P("doc", "vocab", None, None),
        ),
        out_specs=(P("vocab", "doc", None), P("doc", None)),
        check_vma=False,
    )
```
